32 devices in a mesh: dp: 4 (over y, x), expert: 8 (over z, core).
Axes of the slice: x: 2, y: 2, z: 4, core: 2. Of those that a mesh axis runs over, the one named last changes fastest.
Arguments:
- tokens: bfloat16 [4096, 1024], P(('dp', 'expert')), may hold values from -12 to 12
- routes: int32 [4096, 8], P(('dp', 'expert')), may hold values from 0 to 31, all different within a row; in each aligned block of 128 rows (0 to 127, 128 to 255, ...) at most 48 rows name the same one
- gate_weights: float32 [4096, 8], P(('dp', 'expert')), may hold values from 0.05 to 0.25
- cotangent: bfloat16 [4096, 1024], P(('dp', 'expert')), may hold values from -12 to 12
- w_gate_up: bfloat16 [1024, 32, 768], P(None, 'expert'), may hold values from -0.1875 to 0.1875
- w_down: bfloat16 [1024, 32, 384], P(None, 'expert'), may hold values from -0.3125 to 0.3125
Outputs:
- layer_out: bfloat16 [4096, 1024], P(('dp', 'expert'))
- grad_tokens: bfloat16 [4096, 1024], P(('dp', 'expert'))
- grad_gate_up: bfloat16 [1024, 32, 768], P('dp', 'expert')
- grad_down: bfloat16 [1024, 32, 384], P('dp', 'expert')
The draws below stay inside these ranges and needn't reach their ends.
Inputs may be any that keep to these rules, and one draw needn't show every extreme that they name: `routes`: each row names 8 different experts. Among the 128 rows of one device no expert is named more than 48 times, and in some device's rows an expert is named exactly 48 times.
All inputs are finite; a program needn't handle non-finite values.
Results may differ from the reference program's by a relative error of at most 0.015.
Values may be sent and summed in bfloat16 or wider, within the bound.
No kernel may reach another device: no remote copies, remote signals or barrier semaphores. Data moves between devices by JAX's collectives and lax.ppermute only.
A program may use at most 128 MiB of HBM per device.

```python
import math
import jax
import jax.numpy as jnp
import numpy as np
from jax import lax

D = 1024
H = 384
TOP = 8
TOK_DEV = 128
EXPERTS = 32
TOKENS = 4096
MOST = 48
N_DP = 4
N_EXPERT = 8


def spiked(array, own_key, source, target, blocks, factor):
    def block_of(dim):
        return (jnp.arange(array.shape[dim]) // (array.shape[dim] // blocks)).reshape((-1,) + (1,) * (array.ndim - 1 - dim))

    one_side = jax.random.permutation(own_key, blocks)[block_of(target)]
    far = (block_of(target) + blocks // 2) % blocks
    return jnp.where((block_of(source) == one_side) | (block_of(source) == far), factor * array, array)


def block_scale(rng, shape, pieces, least, top_value):
    level, own = 1.0, jax.random.fold_in(rng, 6)
    for dim, blocks in pieces:
        draws = jnp.exp(jax.random.uniform(jax.random.fold_in(own, dim), (blocks,), jnp.float32, least / len(pieces), top_value / len(pieces)))
        level = level * jnp.repeat(draws, shape[dim] // blocks).reshape([-1 if axis == dim else 1 for axis in range(len(shape))])
    return level


def routed_block(rng, own, number, rows, amount, top, limit, skew):
    ranking = jax.random.permutation(rng, amount)
    heavy_load, usual = shares(amount, rows * top, limit, skew, True), shares(amount, rows * top, limit, skew, False)
    places = jnp.arange(amount)

    def named(sizes, turn):
        used = int((sizes > 0).sum())
        fixed = max(1, used // 4)
        passed = fixed + (places - fixed + turn * (used - fixed)) % max(1, amount - fixed)
        return jnp.zeros((amount,), jnp.int32).at[ranking[jnp.where(places < fixed, places, passed)]].set(jnp.asarray(sizes, jnp.int32))

    sizes = jnp.where(number % 4 == 0, named(heavy_load, number // 4), named(usual, number - number // 4 - 1))
    mixed = jax.random.permutation(jax.random.fold_in(own, 3), amount)
    giver, taker = mixed[0:amount // 2 * 2:2], mixed[1:amount // 2 * 2:2]
    slack = jnp.minimum(sizes[giver] - 1, limit - sizes[taker]) // 2
    slack = jnp.where((giver == ranking[0]) | (taker == ranking[0]) | (sizes[taker] == 0), 0, jnp.maximum(slack, 0))
    passed = jax.random.randint(jax.random.fold_in(own, 4), (amount // 2,), 0, 1 << 20) % (slack + 1)
    sizes = sizes.at[giver].add(-passed).at[taker].add(passed)
    items = jnp.searchsorted(jnp.cumsum(sizes), jnp.arange(rows * top), side="right").astype(jnp.int32)
    listing = items.reshape(top, rows).T
    listing = listing[jax.random.permutation(jax.random.fold_in(own, 1), rows)]
    turn = jax.random.randint(jax.random.fold_in(own, 2), (rows, 1), 0, top)
    return jnp.take_along_axis(listing, (jnp.arange(top)[None, :] + turn) % top, axis=1)


def shares(amount, total, most, lean, full):
    weights = [(1 << 20) // math.isqrt(rank ** lean) + 1 for rank in range(1, amount + 1)]
    largest = most if full else min(most, max(-(-total // amount), total * weights[0] // sum(weights)))
    least = 1 if total - largest >= amount - 1 else 0
    counts, spare = [largest] + [least] * (amount - 1), total - largest - least * (amount - 1)
    while spare > 0:
        candidates = [i for i in range(1, amount) if counts[i] < largest] or [i for i in range(1, amount) if counts[i] < most]
        whole, budget = sum([weights[i] for i in candidates]), spare
        for i in candidates:
            extra = min(most - counts[i], max(1, budget * weights[i] // whole), spare)
            counts[i] = counts[i] + extra
            spare = spare - extra
    return np.array(counts)


def bell_draw(key, extent, spread, most, pieces=(), kind=jnp.bfloat16):
    values = spread * jax.random.normal(key, extent, jnp.float32)
    if pieces:
        values = values * block_scale(key, extent, pieces, -0.22, 0.18)
    return jnp.clip(values, -most, most).astype(kind)


def heavy_noise(own_key, extent, deviation, reach, cuts, heavy, kind=jnp.bfloat16):
    entries = deviation * jax.random.normal(own_key, extent, jnp.float32)
    if cuts:
        entries = entries * block_scale(own_key, extent, cuts, -0.22, 0.18)
    return jnp.clip(spiked(entries, jax.random.fold_in(own_key, 3), *heavy), -reach, reach).astype(kind)


def setup_inputs(seed: int = 0) -> dict:
    seeds = jax.random.split(jax.random.key(seed), 7)
    tokens = heavy_noise(seeds[0], (TOKENS, D), 1.0, 12.0, ((0, 32),), (0, 1, 32, 2.75))
    routes_keys = jax.random.split(jax.random.fold_in(seeds[1], 1), TOKENS // TOK_DEV)
    routes_turns = jax.random.permutation(jax.random.fold_in(seeds[1], 3), TOKENS // TOK_DEV)
    routes = jax.vmap(lambda own, number: routed_block(jax.random.fold_in(seeds[1], 2), own, number, TOK_DEV, EXPERTS, TOP, MOST, 2))(routes_keys, routes_turns).reshape((TOKENS, TOP))
    gate_weights = jnp.clip(0.05 + 0.2 * jax.random.uniform(seeds[2], (TOKENS, TOP), jnp.float32) ** block_scale(seeds[2], (TOKENS, TOP), ((0, 32),), -0.2, 0.2), 0.05, 0.25)
    cotangent = heavy_noise(seeds[3], (TOKENS, D), 1.0, 12.0, ((0, 32),), (0, 1, 32, 2.75))
    w_gate_up = bell_draw(seeds[4], (D, EXPERTS, 2 * H), D ** -0.5, 0.1875, ((1, 8),))
    w_down = bell_draw(seeds[5], (D, EXPERTS, H), H ** -0.5, 0.3125, ((1, 8),))
    return dict(tokens=tokens, routes=routes, gate_weights=gate_weights, cotangent=cotangent, w_gate_up=w_gate_up, w_down=w_down)


def split_parts(projected, hidden_units):
    gate_part = projected[..., :hidden_units]
    up_part = projected[..., hidden_units:]
    sigma = jax.nn.sigmoid(gate_part)
    return gate_part, up_part, sigma


def reference(tokens, routes, gate_weights, cotangent, w_gate_up, w_down):
    group_rows = TOK_DEV * N_EXPERT
    capacity = N_EXPERT * MOST
    assigned = group_rows * TOP
    slots_all = EXPERTS * capacity
    weights_gu = w_gate_up.astype(jnp.float32)
    weights_dn = w_down.astype(jnp.float32)

    def one_group(carry, operands):
        x_rows, route_rows, gate_rows, cot_rows = operands
        flat_routes = route_rows.reshape(assigned).astype(jnp.int32)
        onehot = (flat_routes[:, None] == jnp.arange(EXPERTS, dtype=jnp.int32)[None, :]).astype(jnp.int32)
        slot_rank = jnp.sum((jnp.cumsum(onehot, axis=0) - 1) * onehot, axis=1).astype(jnp.int32)
        slot_index = (flat_routes * capacity + slot_rank).astype(jnp.int32)
        source_of = jnp.zeros((slots_all,), jnp.int32).at[slot_index].set(jnp.arange(assigned, dtype=jnp.int32))
        filled = jnp.zeros((slots_all,), jnp.int32).at[slot_index].set(1) > 0
        token_of = (source_of // TOP).astype(jnp.int32)
        x_slots = jnp.where(filled[:, None], x_rows[token_of], 0).reshape(EXPERTS, capacity, D)
        projected = jnp.einsum('ecd,def->ecf', x_slots.astype(jnp.float32), weights_gu)
        gate_part, up_part, sigma = split_parts(projected, H)
        hidden = (gate_part * sigma * up_part).astype(jnp.bfloat16)
        expert_out = jnp.einsum('ech,deh->ecd', hidden.astype(jnp.float32), weights_dn).astype(jnp.bfloat16)
        per_assign = expert_out.reshape(slots_all, D)[slot_index].astype(jnp.float32).reshape(group_rows, TOP, D)
        layer_out = jnp.sum(per_assign * gate_rows[:, :, None], axis=1).astype(jnp.bfloat16)
        weighted = (gate_rows[:, :, None] * cot_rows.astype(jnp.float32)[:, None, :]).astype(jnp.bfloat16)
        weighted = weighted.reshape(assigned, D)
        cot_slots = jnp.where(filled[:, None], weighted[source_of], 0).reshape(EXPERTS, capacity, D)
        d_hidden = jnp.einsum('ecd,deh->ech', cot_slots.astype(jnp.float32), weights_dn)
        d_gate = d_hidden * up_part * sigma * (1.0 + gate_part * (1.0 - sigma))
        d_up = d_hidden * gate_part * sigma
        d_proj = jnp.concatenate([d_gate, d_up], axis=-1).astype(jnp.bfloat16)
        slot_grads = jnp.einsum('ecf,def->ecd', d_proj.astype(jnp.float32), weights_gu).astype(jnp.bfloat16)
        grad_assign = slot_grads.reshape(slots_all, D)[slot_index].astype(jnp.float32).reshape(group_rows, TOP, D)
        grad_rows = jnp.sum(grad_assign, axis=1).astype(jnp.bfloat16)
        part_gu = jnp.einsum('ecd,ecf->def', x_slots.astype(jnp.float32), d_proj.astype(jnp.float32)).astype(jnp.bfloat16)
        part_dn = jnp.einsum('ecd,ech->deh', cot_slots.astype(jnp.float32), hidden.astype(jnp.float32)).astype(jnp.bfloat16)
        summed_gu, summed_dn = carry
        carry = (summed_gu + part_gu.astype(jnp.float32), summed_dn + part_dn.astype(jnp.float32))
        return carry, (layer_out, grad_rows)

    start_carry = (jnp.zeros((D, EXPERTS, 2 * H), jnp.float32), jnp.zeros((D, EXPERTS, H), jnp.float32))
    operands = (tokens.reshape(N_DP, group_rows, D), routes.reshape(N_DP, group_rows, TOP),
                gate_weights.reshape(N_DP, group_rows, TOP), cotangent.reshape(N_DP, group_rows, D))
    totals, stacked = lax.scan(one_group, start_carry, operands)
    layer_out = stacked[0].reshape(TOKENS, D)
    grad_tokens = stacked[1].reshape(TOKENS, D)
    return layer_out, grad_tokens, totals[0].astype(jnp.bfloat16), totals[1].astype(jnp.bfloat16)
```

```python
import jax
import jax.numpy as jnp
from jax import lax
from jax.experimental import pallas as pl
from jax.experimental.pallas import tpu as pltpu
from jax.sharding import PartitionSpec as P

CORES = 2
BF = jnp.bfloat16
F32 = jnp.float32
VMEM = 56 * 1024 * 1024


def dot(a, b):
    return lax.dot_general(a, b, (((1,), (0,)), ((), ())), preferred_element_type=F32)


def dot_t(a, b):
    return lax.dot_general(a, b, (((1,), (1,)), ((), ())), preferred_element_type=F32)


def from_further(k, peers):
    chips = peers // CORES
    return [(((z + k) % chips) * CORES + c, z * CORES + c) for z in range(chips) for c in range(CORES)]


def to_further(k, peers):
    return [(dst, src) for src, dst in from_further(k, peers)]


def partner(peers):
    return [(i, i ^ 1) for i in range(peers)]


def gather_slots(x, peers):
    chips = peers // CORES
    own = [x] + [lax.ppermute(x, "expert", from_further(k, peers)) for k in range(1, chips)]
    own = jnp.stack(own)
    other = lax.ppermute(own, "expert", partner(peers))
    return jnp.concatenate([own, other], axis=0)


def scatter_slots(own, other, peers, gate=None):
    chips = peers // CORES
    rows = own.shape[0] // chips
    got = lax.ppermute(other, "expert", partner(peers))

    def part(k):
        a = lax.slice_in_dim(own, k * rows, (k + 1) * rows, axis=0).astype(F32)
        return a + lax.slice_in_dim(got, k * rows, (k + 1) * rows, axis=0).astype(F32)

    total = part(0)
    arrived = [lax.ppermute(part(k).astype(BF), "expert", to_further(k, peers)) for k in range(1, chips)]
    for piece in arrived:
        total = total + piece.astype(F32)
    return total.astype(BF)


def transpose(x):
    rows, width = x.shape
    step = min(256, width)

    def kern(x_ref, o_ref):
        o_ref[...] = x_ref[...].T

    return pl.pallas_call(
        kern,
        grid=(width // step,),
        in_specs=[pl.BlockSpec((rows, step), lambda i: (0, i))],
        out_specs=pl.BlockSpec((step, rows), lambda i: (i, 0)),
        out_shape=jax.ShapeDtypeStruct((width, rows), x.dtype),
        compiler_params=pltpu.CompilerParams(vmem_limit_bytes=VMEM),
        name="turn",
    )(x)


def gate_column(gates, e):
    lane = lax.broadcasted_iota(jnp.int32, gates.shape, 1)
    return jnp.sum(jnp.where(lane == e, gates, 0.0), axis=1, keepdims=True)


def forward(x, gates, w_gu, w_dn):
    rows, width = x.shape
    exp_dev, _, hid = w_dn.shape
    tile = min(256, rows)
    steps = rows // tile

    def kern(x_ref, g_ref, wgu_ref, wdn_ref, fac_ref, own_ref, other_ref, acc_ref):
        e, i = pl.program_id(0), pl.program_id(1)
        proj = dot(x_ref[...], wgu_ref[0])
        gate = gate_column(g_ref[...], e)
        g, u = proj[:, :hid], proj[:, hid:]
        s = jax.nn.sigmoid(g)
        gs = g * s
        gh = (gate * (gs * u)).astype(BF)
        fac_ref[0, :, :hid] = (gate * (u * s * (1.0 + g * (1.0 - s)))).astype(BF)
        fac_ref[0, :, hid : 2 * hid] = (gate * gs).astype(BF)
        fac_ref[0, :, 2 * hid :] = gh
        out = dot_t(gh, wdn_ref[0])
        here = pl.ds(i * tile, tile)

        @pl.when(e == 0)
        def _():
            acc_ref[here, :] = out

        @pl.when(e > 0)
        def _():
            acc_ref[here, :] = acc_ref[here, :] + out

        @pl.when((e == exp_dev - 1) & (i < steps // 2))
        def _():
            own_ref[here, :] = acc_ref[here, :].astype(BF)

        @pl.when((e == exp_dev - 1) & (i >= steps // 2))
        def _():
            other_ref[pl.ds((i - steps // 2) * tile, tile), :] = acc_ref[here, :].astype(BF)

    half = jax.ShapeDtypeStruct((rows // 2, width), BF)
    return pl.pallas_call(
        kern,
        grid=(exp_dev, steps),
        in_specs=[
            pl.BlockSpec((tile, width), lambda e, i: (i, 0)),
            pl.BlockSpec((tile, exp_dev), lambda e, i: (i, 0)),
            pl.BlockSpec((1, width, 2 * hid), lambda e, i: (e, 0, 0)),
            pl.BlockSpec((1, width, hid), lambda e, i: (e, 0, 0)),
        ],
        out_specs=[
            pl.BlockSpec((1, tile, 3 * hid), lambda e, i: (e, i, 0)),
            pl.BlockSpec((rows // 2, width), lambda e, i: (0, 0)),
            pl.BlockSpec((rows // 2, width), lambda e, i: (0, 0)),
        ],
        out_shape=[jax.ShapeDtypeStruct((exp_dev, rows, 3 * hid), BF), half, half],
        scratch_shapes=[pltpu.VMEM((rows, width), F32)],
        compiler_params=pltpu.CompilerParams(vmem_limit_bytes=VMEM),
        name="forward",
    )(x, gates, w_gu, w_dn)


def weight_grads(e, blocks, sub, c, w_dn, fac, xt, ct):
    rows, width = c.shape
    hid = w_dn.shape[2]
    quarter = width // 4
    small = quarter // sub
    tile = min(256, rows)
    steps = rows // tile

    def kern(b_ref, c_ref, wdn_ref, fac_ref, gh_ref, *rest):
        xts, cts = rest[:sub], rest[sub : 2 * sub]
        outs, dp_out, dp_ref = rest[2 * sub : 2 * sub + 4], rest[2 * sub + 4], rest[2 * sub + 5]
        i = pl.program_id(0)

        @pl.when(i < steps)
        def _():
            dh = dot(c_ref[...], wdn_ref[0])
            here = pl.ds(i * tile, tile)
            d_gate = (dh * fac_ref[0, :, :hid].astype(F32)).astype(BF)
            d_up = (dh * fac_ref[0, :, hid:].astype(F32)).astype(BF)
            dp_ref[here, :hid] = d_gate
            dp_ref[here, hid:] = d_up
            dp_out[:, :hid] = d_gate
            dp_out[:, hid:] = d_up

        for q in range(4):

            @pl.when(i == steps + q)
            def _():
                lhs = jnp.concatenate([r[...] for r in xts], axis=0)
                outs[q][:, : 2 * hid] = dot(lhs, dp_ref[...]).astype(BF)
                lhs = jnp.concatenate([r[...] for r in cts], axis=0)
                outs[q][:, 2 * hid :] = dot(lhs, gh_ref[0]).astype(BF)

    def row(i, b):
        return jnp.minimum(i, steps - 1)

    def turned(k):
        return pl.BlockSpec((small, rows), lambda i, b: (b[jnp.maximum(i - steps, 0) * sub + k], 0))

    piece = jax.ShapeDtypeStruct((quarter, 3 * hid), BF)
    return pl.pallas_call(
        kern,
        grid_spec=pltpu.PrefetchScalarGridSpec(
            num_scalar_prefetch=1,
            grid=(steps + 4,),
            in_specs=[
                pl.BlockSpec((tile, width), lambda i, b: (row(i, b), 0)),
                pl.BlockSpec((1, width, hid), lambda i, b: (e, 0, 0)),
                pl.BlockSpec((1, tile, 2 * hid), lambda i, b: (e, row(i, b), 0)),
                pl.BlockSpec((1, rows, hid), lambda i, b: (e, 0, 2)),
            ]
            + [turned(k) for k in range(sub)] * 2,
            out_specs=[pl.BlockSpec((quarter, 3 * hid), lambda i, b: (0, 0))] * 4
            + [pl.BlockSpec((tile, 2 * hid), lambda i, b: (row(i, b), 0))],
            scratch_shapes=[pltpu.VMEM((rows, 2 * hid), BF)],
        ),
        out_shape=[piece] * 4 + [jax.ShapeDtypeStruct((rows, 2 * hid), BF)],
        compiler_params=pltpu.CompilerParams(vmem_limit_bytes=VMEM),
        name=f"weight_grads_{e}",
    )(blocks, c, w_dn, fac, fac, *([xt] * sub), *([ct] * sub))


def token_grads(d_proj, w_gu):
    exp_dev = len(d_proj)
    rows, wide = d_proj[0].shape
    width = w_gu.shape[1]
    tile = min(256, rows)
    steps = rows // tile

    def kern(*refs):
        dps, w_ref, own_ref, other_ref = refs[:exp_dev], refs[exp_dev], refs[exp_dev + 1], refs[exp_dev + 2]
        i = pl.program_id(0)
        acc = dot_t(dps[0][...], w_ref[0])
        for e in range(1, exp_dev):
            acc = acc + dot_t(dps[e][...], w_ref[e])

        @pl.when(i < steps // 2)
        def _():
            own_ref[...] = acc.astype(BF)

        @pl.when(i >= steps // 2)
        def _():
            other_ref[...] = acc.astype(BF)

    half = jax.ShapeDtypeStruct((rows // 2, width), BF)
    return pl.pallas_call(
        kern,
        grid=(steps,),
        in_specs=[pl.BlockSpec((tile, wide), lambda i: (i, 0))] * exp_dev
        + [pl.BlockSpec((exp_dev, width, wide), lambda i: (0, 0, 0), pipeline_mode=pl.Buffered(1))],
        out_specs=[
            pl.BlockSpec((tile, width), lambda i: (jnp.minimum(i, steps // 2 - 1), 0)),
            pl.BlockSpec((tile, width), lambda i: (jnp.maximum(i - steps // 2, 0), 0)),
        ],
        out_shape=[half, half],
        compiler_params=pltpu.CompilerParams(vmem_limit_bytes=VMEM),
        name="token_grads",
    )(*d_proj, w_gu)


def reduce_groups(keep, send, bits, groups):
    for n, bit in enumerate(bits):
        got = lax.ppermute(send, "dp", [(i, i ^ (1 << bit)) for i in range(groups)])
        total = keep.astype(F32) + got.astype(F32)
        if n == len(bits) - 1:
            return total.astype(BF)
        half = keep.shape[0] // 2
        keep, send = total[:half].astype(BF), total[half:].astype(BF)


def per_device(tokens, routes, gate_weights, cotangent, w_gate_up, w_down):
    tok_dev, active = routes.shape
    width = tokens.shape[1]
    exp_dev = w_down.shape[1]
    hid = w_down.shape[2]
    peers = lax.axis_size("expert")
    groups = lax.axis_size("dp")
    rows = tok_dev * peers
    n_bits = groups.bit_length() - 1
    orders = (tuple(range(n_bits)), tuple(reversed(range(n_bits))))

    x = gather_slots(tokens, peers).reshape(rows, width)
    small = jnp.concatenate([routes.T.astype(F32), gate_weights.T], axis=0)
    small = gather_slots(small, peers)
    c = gather_slots(cotangent, peers).reshape(rows, width)

    first = lax.axis_index("expert") * exp_dev
    named = small[:, :active, :].astype(jnp.int32)
    mine = first + jnp.arange(exp_dev, dtype=jnp.int32)
    hit = named[:, :, :, None] == mine
    gates = jnp.sum(jnp.where(hit, small[:, active:, :, None], 0.0), axis=1).reshape(rows, exp_dev)

    w_gu = jnp.transpose(w_gate_up, (1, 0, 2))
    w_dn = jnp.transpose(w_down, (1, 0, 2))

    me = lax.axis_index("dp")
    sub = max(1, groups // 2)
    blocks = []
    for want in (1, 0):
        for colour, order in enumerate(orders):
            for pos in range(groups // 2):
                full = pos + want * (groups // 2)
                rel = sum(((full >> (n_bits - 1 - n)) & 1) << bit for n, bit in enumerate(order))
                blocks.append((me ^ rel) * 2 + colour)
    blocks = jnp.stack(blocks).astype(jnp.int32)

    fac, out_own, out_other = forward(x, gates, w_gu, w_dn)
    xt = transpose(x)
    ct = transpose(c)
    d_proj, reduced = [], []
    for e in range(exp_dev):
        send_a, send_b, keep_a, keep_b, dp = weight_grads(e, blocks, sub, c, w_dn, fac, xt, ct)
        d_proj.append(dp)
        part_a = reduce_groups(keep_a, send_a, orders[0], groups)
        part_b = reduce_groups(keep_b, send_b, orders[1], groups)
        reduced.append(jnp.concatenate([part_a, part_b], axis=0))
    grad_own, grad_other = token_grads(d_proj, w_gu)
    layer_out = scatter_slots(out_own, out_other, peers)
    grad_tokens = scatter_slots(grad_own, grad_other, peers)
    summed = jnp.stack(reduced, axis=1)
    return (layer_out, grad_tokens, summed[:, :, : 2 * hid], summed[:, :, 2 * hid :])


def solution(mesh):
    rows = P(("dp", "expert"), None)
    return jax.shard_map(
        per_device,
        mesh=mesh,
        in_specs=(rows, rows, rows, rows, P(None, "expert", None), P(None, "expert", None)),
        out_specs=(rows, rows, P("dp", "expert", None), P("dp", "expert", None)),
        check_vma=False,
    )
```
